32 devices in a mesh: groups: 2 (over x), row: 16 (over z, y, core).
Axes of the slice: x: 2, y: 2, z: 4, core: 2. Of those that a mesh axis runs over, the one named last changes fastest.
Arguments:
- coupling: bfloat16 [32768, 896], P(('groups', 'row')), parts along dimension 0, may hold values from -6 to 6
- column_block: bfloat16 [32768, 1536], P(('groups', 'row')), parts along dimension 0, may hold values from -6 to 6
- pivot_inverse: bfloat16 [3072, 1536], P(('groups', 'row')), parts along dimension 0, may hold values from -0.15625 to 0.15625
- row_panel: bfloat16 [1536, 1792], P(None, ('groups', 'row')), parts along dimension 1, may hold values from -0.15625 to 0.15625
Outputs:
- lower_panel: bfloat16 [32768, 1536], P(('groups', 'row')), parts along dimension 0
- schur: bfloat16 [32768, 896], P(('groups', 'row')), parts along dimension 0
The draws below stay inside these ranges and needn't reach their ends.
There are 2 independent parts, one for each index of `groups`. The reference program is written for one: setup_inputs(seed, part) draws one part's arguments, and reference() takes and returns one part's arrays. A program takes and returns all parts, laid end to end along the dimension named above; each array names one. Nothing has to cross between parts.
All inputs are finite; a program needn't handle non-finite values.
Results may differ from the reference program's by a relative error of at most 0.0039.
Values may be sent and summed in bfloat16 or wider, within the bound.
No kernel may reach another device: no remote copies, remote signals or barrier semaphores. Data moves between devices by JAX's collectives and lax.ppermute only.
A program may use at most 64 MiB of HBM per device.

```python
import jax
import jax.numpy as jnp

K = 1536
COLS = 896
N = 16384


def levels(rng, extent, cuts, smallest, largest):
    loudness = 1.0
    for dim, shards_of in cuts:
        draws = jax.random.uniform(jax.random.fold_in(jax.random.fold_in(rng, 6), dim), (shards_of,), jnp.float32, smallest / len(cuts), largest / len(cuts))
        loudness = loudness * jnp.repeat(jnp.exp(draws), extent[dim] // shards_of).reshape((-1,) + (1,) * (len(extent) - 1 - dim))
    return loudness


def centred(key, dims, deviation, reach, pieces=(), kind=jnp.bfloat16):
    values = jax.random.normal(key, dims, jnp.float32) * deviation
    if len(pieces) > 0:
        values = levels(key, dims, pieces, -0.22, 0.18) * values
    return jnp.clip(values, min=-reach, max=reach).astype(kind)


def setup_inputs(seed: int = 0, part: int = 0) -> dict:
    streams_of = jax.random.split(jax.random.key(seed), 5)
    part_keys = jax.random.split(jax.random.fold_in(streams_of[4], part), 5)
    return {
        "coupling": centred(part_keys[0], (N, COLS), 1.0, 6.0, ((0, 16),)),
        "column_block": centred(part_keys[1], (N, K), 1.0, 6.0, ((0, 16),)),
        "pivot_inverse": centred(part_keys[2], (K, K), K ** -0.5, 0.15625, ((0, 16),)),
        "row_panel": centred(part_keys[3], (K, COLS), K ** -0.5, 0.15625, ((1, 16),)),
    }


def reference(coupling, column_block, pivot_inverse, row_panel):
    lower_panel = jnp.dot(column_block, pivot_inverse, preferred_element_type=jnp.float32).astype(jnp.bfloat16)
    product = jnp.dot(lower_panel, row_panel, preferred_element_type=jnp.float32)
    schur = (coupling.astype(jnp.float32) - product).astype(jnp.bfloat16)
    return (lower_panel, schur)
```

```python
import functools

import jax
import jax.numpy as jnp
from jax import lax
from jax.experimental import pallas as pl
from jax.experimental.pallas import tpu as pltpu
from jax.sharding import PartitionSpec as P

F32, BF16 = jnp.float32, jnp.bfloat16
ON_CHIP = pl.BlockSpec(memory_space=pltpu.VMEM)
IN_PLACE = pl.BlockSpec(memory_space=pl.ANY)
PARAMS = pltpu.CompilerParams(vmem_limit_bytes=40 << 20)


def shape(*dims):
    return jax.ShapeDtypeStruct(dims, BF16)


def cost(flops, nbytes):
    return pl.CostEstimate(flops=flops, bytes_accessed=nbytes, transcendentals=0)


def ring_of(chips):
    if chips > 8:
        return list(range(chips))
    return list(range(0, chips, 2)) + list(range(chips - 1, 0, -2))


def distances(chips):
    near = [0]
    for k in range(1, (chips + 1) // 2):
        near += [-k, k]
    return near + ([chips // 2] if chips % 2 == 0 else [])


def chip_at(distance, chips):
    chip = lax.axis_index("row") // 2
    if chips > 8:
        return lax.rem(chip + distance + chips, chips)
    place = jnp.where(lax.rem(chip, 2) == 0, chip // 2, chips - 1 - chip // 2)
    place = lax.rem(place + distance + chips, chips)
    return jnp.where(place < chips // 2, 2 * place, 2 * (chips - 1 - place) + 1)


def my_core():
    return lax.rem(lax.axis_index("row"), 2)


def split_kernel(shard, mine, theirs):
    half = mine.shape[1]
    first = my_core() == 0
    left, right = shard[:, :half], shard[:, half:]
    mine[...] = jnp.where(first, left, right)
    theirs[...] = jnp.where(first, right, left)


def split(shard):
    rows, cols = shard.shape
    return pl.pallas_call(
        split_kernel,
        out_shape=(shape(rows, cols // 2),) * 2,
        in_specs=[ON_CHIP],
        out_specs=(ON_CHIP, ON_CHIP),
        compiler_params=PARAMS,
        name="split",
    )(shard)


def place_kernel(chips, *refs):
    pieces, whole, sems = refs[:-2], refs[-2], refs[-1]
    rows = pieces[0].shape[0]
    copies = []
    for i, distance in enumerate(distances(chips)):
        chip = chip_at(distance, chips)
        for stream in range(2):
            core = my_core() if stream == 0 else 1 - my_core()
            at = pl.multiple_of((2 * chip + core) * rows, 8)
            j = 2 * i + stream
            copies.append(pltpu.make_async_copy(pieces[j], whole.at[pl.ds(at, rows)], sems.at[j]))
    for copy in copies:
        copy.start()
    for copy in copies:
        copy.wait()


def place(pieces, chips, name):
    rows, cols = pieces[0].shape
    return pl.pallas_call(
        functools.partial(place_kernel, chips),
        out_shape=shape(rows * len(pieces), cols),
        in_specs=[ON_CHIP] * len(pieces),
        out_specs=ON_CHIP,
        scratch_shapes=[pltpu.SemaphoreType.DMA((len(pieces),))],
        compiler_params=PARAMS,
        cost_estimate=cost(0, 4 * rows * len(pieces) * cols),
        name=name,
    )(*pieces)


def lower_kernel(own, *refs):
    column, panel = refs[:2]
    out, kept, sems = refs[-3:]
    half = panel.shape[1]
    core = my_core() if own else 1 - my_core()
    cols = pl.ds(pl.multiple_of(core * half, 128), half)
    rows = column.shape[0] // 4
    copies = []
    for i in range(4):
        at = pl.ds(i * rows, rows)
        kept[at] = jnp.dot(column[at], panel[...], preferred_element_type=F32).astype(BF16)
        copies.append(pltpu.make_async_copy(kept.at[at], out.at[at, cols], sems.at[i]))
        copies[-1].start()
    for copy in copies:
        copy.wait()


def lower(column_block, panel, so_far):
    own = so_far is None
    n, k = column_block.shape
    half = panel.shape[1]
    return pl.pallas_call(
        functools.partial(lower_kernel, own),
        out_shape=(shape(n, 2 * half), shape(n, half)),
        in_specs=[ON_CHIP, ON_CHIP] + ([] if own else [IN_PLACE]),
        out_specs=(IN_PLACE, ON_CHIP),
        scratch_shapes=[pltpu.SemaphoreType.DMA((4,))],
        input_output_aliases={} if own else {2: 0},
        compiler_params=PARAMS,
        cost_estimate=cost(2 * n * k * half, 2 * (n * k + k * half + n * half)),
        name="lower_own" if own else "lower_other",
    )(column_block, panel, *([] if own else [so_far]))


def schur_kernel(own_lower, own_panel, other_lower, other_panel, coupling, out, done, sems):
    rows = coupling.shape[0] // 4
    contract = (((1,), (1,)), ((), ()))
    copies = []
    for i in range(4):
        at = pl.ds(i * rows, rows)
        product = lax.dot_general(own_lower[at], own_panel[...], contract, preferred_element_type=F32)
        product += lax.dot_general(other_lower[at], other_panel[...], contract, preferred_element_type=F32)
        done[at] = (coupling[at].astype(F32) - product).astype(BF16)
        copies.append(pltpu.make_async_copy(done.at[at], out.at[at], sems.at[i]))
        copies[-1].start()
    for copy in copies:
        copy.wait()


def schur(own_lower, own_panel, other_lower, other_panel, coupling):
    n, cols = coupling.shape
    k = 2 * own_lower.shape[1]
    return pl.pallas_call(
        schur_kernel,
        out_shape=shape(n, cols),
        in_specs=[ON_CHIP] * 5,
        out_specs=IN_PLACE,
        scratch_shapes=[pltpu.VMEM((n, cols), BF16), pltpu.SemaphoreType.DMA((4,))],
        compiler_params=PARAMS,
        cost_estimate=cost(2 * n * k * cols, 2 * (n * k + k * cols + 2 * n * cols)),
        name="schur",
    )(own_lower, own_panel, other_lower, other_panel, coupling)


def gather_half(shard, chips, up, down, swap):
    mine, theirs = split(shard)
    rising = [mine, lax.ppermute(theirs, "row", swap)]
    falling = list(rising)
    got = {(s, 0): rising[s] for s in range(2)}
    for k in range(1, chips // 2 + 1):
        last = 2 * k == chips
        for s in range(2):
            if not (last and s == 1):
                rising[s] = lax.ppermute(rising[s], "row", up)
                got[s, k if last else -k] = rising[s]
            if not (last and s == 0):
                falling[s] = lax.ppermute(falling[s], "row", down)
                got[s, k] = falling[s]
    return [got[s, d] for d in distances(chips) for s in range(2)]


def on_device(devices, coupling, column_block, pivot_inverse, row_panel):
    chips = devices // 2
    ring = ring_of(chips)
    swap = [(i, i ^ 1) for i in range(devices)]
    up = [(2 * ring[i] + c, 2 * ring[(i + 1) % chips] + c) for i in range(chips) for c in range(2)]
    down = [(to, at) for at, to in up]
    pieces = gather_half(pivot_inverse, chips, up, down, swap)
    own_p = place(pieces, chips, "place_p")
    shard, gate = lax.optimization_barrier((row_panel.T, pieces[2 * (chips - 4)]))
    own_r = place(gather_half(shard, chips, up, down, swap), chips, "place_r")
    other_p = lax.ppermute(own_p, "row", swap)
    other_r = lax.ppermute(own_r, "row", swap)
    lower_panel, own_lower = lower(column_block, own_p, None)
    lower_panel, other_lower = lower(column_block, other_p, lower_panel)
    return lower_panel, schur(own_lower, own_r, other_lower, other_r, coupling)


def by_all_gather(coupling, column_block, pivot_inverse, row_panel):
    whole_inverse = lax.all_gather(pivot_inverse, "row", axis=0, tiled=True)
    whole_panel = lax.all_gather(row_panel, "row", axis=1, tiled=True)
    lower_panel = jnp.dot(column_block, whole_inverse, preferred_element_type=F32).astype(BF16)
    product = jnp.dot(lower_panel, whole_panel, preferred_element_type=F32)
    return lower_panel, (coupling.astype(F32) - product).astype(BF16)


def solution(mesh):
    devices = mesh.shape["row"]
    parts = mesh.shape["groups"]

    def step(coupling, column_block, pivot_inverse, row_panel):
        aligned = row_panel.shape[1] // (parts * devices) % 8 == 0
        aligned &= pivot_inverse.shape[0] // (parts * devices) % 8 == 0
        body = functools.partial(on_device, devices) if aligned else by_all_gather
        rows = P(("groups", "row"), None)
        return jax.shard_map(
            body,
            mesh=mesh,
            in_specs=(rows, rows, rows, P(None, ("groups", "row"))),
            out_specs=(rows, rows),
            check_vma=False,
        )(coupling, column_block, pivot_inverse, row_panel)

    return step
```

```python
import functools

import jax
import jax.numpy as jnp
from jax import lax
from jax.experimental import pallas as pl
from jax.experimental.pallas import tpu as pltpu
from jax.sharding import PartitionSpec as P

F32, BF16 = jnp.float32, jnp.bfloat16
ON_CHIP = pl.BlockSpec(memory_space=pltpu.VMEM)
IN_HBM = pl.BlockSpec(memory_space=pltpu.HBM)
PARAMS = pltpu.CompilerParams(vmem_limit_bytes=16 << 20)
CHUNKS = 4
WEIGHT = 20


def shape(*dims):
    return jax.ShapeDtypeStruct(dims, BF16)


def cost(flops, nbytes):
    return pl.CostEstimate(flops=flops, bytes_accessed=nbytes, transcendentals=0)


def small(kernel, out_shape, operands, name):
    return pl.pallas_call(
        kernel,
        out_shape=out_shape,
        in_specs=[ON_CHIP] * len(operands),
        out_specs=jax.tree.map(lambda _: ON_CHIP, out_shape),
        compiler_params=PARAMS,
        name=name,
    )(*operands)


def in_hbm(x):
    return pltpu.with_memory_space_constraint(x, pltpu.HBM)


def after(value, *others):
    return lax.optimization_barrier((value, *others))[0]


def ring_of(chips):
    if chips > 8:
        return list(range(chips))
    return list(range(0, chips, 2)) + list(range(chips - 1, 0, -2))


def chip_at(distance, chips):
    chip = lax.axis_index("row") // 2
    if chips > 8:
        return lax.rem(chip + distance + chips, chips)
    place = jnp.where(lax.rem(chip, 2) == 0, chip // 2, chips - 1 - chip // 2)
    place = lax.rem(place + distance + chips, chips)
    return jnp.where(place < chips // 2, 2 * place, 2 * (chips - 1 - place) + 1)


def my_core():
    return lax.rem(lax.axis_index("row"), 2)


def split_kernel(inverse, panel, mine, theirs, sems):
    rows, half = inverse.shape[0], mine.shape[1]
    copies = []
    for i, (ref, at) in enumerate(((inverse, pl.ds(0, rows)), (panel, pl.ds(rows, panel.shape[0])))):
        for j, (out, core) in enumerate(((mine, my_core()), (theirs, 1 - my_core()))):
            cols = pl.ds(pl.multiple_of(core * half, 128), half)
            copies.append(pltpu.make_async_copy(ref.at[:, cols], out.at[at], sems.at[2 * j + i]))
            copies[-1].start()
    for copy in copies:
        copy.wait()


def split(inverse, panel):
    out = shape(inverse.shape[0] + panel.shape[0], inverse.shape[1] // 2)
    return pl.pallas_call(
        split_kernel,
        out_shape=(out, out),
        in_specs=[IN_HBM, IN_HBM],
        out_specs=(ON_CHIP, ON_CHIP),
        scratch_shapes=[pltpu.SemaphoreType.DMA((4,))],
        compiler_params=PARAMS,
        name="split",
    )(in_hbm(inverse), in_hbm(panel))


def fetch_kernel(*refs):
    count = len(refs) // 2
    copies = [pltpu.make_async_copy(refs[i], refs[count + i], refs[-1].at[i]) for i in range(count)]
    for copy in copies:
        copy.start()
    for copy in copies:
        copy.wait()


def fetch(*arrays):
    return pl.pallas_call(
        fetch_kernel,
        out_shape=tuple(shape(*x.shape) for x in arrays),
        in_specs=[IN_HBM] * len(arrays),
        out_specs=(ON_CHIP,) * len(arrays),
        scratch_shapes=[pltpu.SemaphoreType.DMA((len(arrays),))],
        compiler_params=PARAMS,
        name="fetch",
    )(*map(in_hbm, arrays))


def stack(parts, name):
    def kernel(*refs):
        to = 0
        for ref, (_, start, rows) in zip(refs, parts):
            refs[-1][to : to + rows] = ref[start : start + rows]
            to += rows

    rows, cols = sum(part[2] for part in parts), parts[0][0].shape[1]
    return small(kernel, shape(rows, cols), [part[0] for part in parts], name)


def place(parts, rows, chips, flip, name):
    def kernel(*refs):
        for ref, (_, start, distance, stream) in zip(refs, parts):
            core = my_core() if stream == flip else 1 - my_core()
            at = pl.multiple_of((2 * chip_at(distance, chips) + core) * rows, 8)
            refs[-1][pl.ds(at, rows), :] = ref[start : start + rows]

    cols = parts[0][0].shape[1]
    return small(kernel, shape(2 * chips * rows, cols), [part[0] for part in parts], name)


def lower_kernel(column, panel, *refs):
    if len(refs) > 1:
        kept, out, lower_out, sem = refs
        half = kept.shape[1]
        cols = pl.ds(pl.multiple_of(my_core() * half, 128), half)
        copy = pltpu.make_async_copy(kept, lower_out.at[:, cols], sem)
        copy.start()
    else:
        out, copy = refs[0], None
    rows = column.shape[0] // CHUNKS
    for i in range(CHUNKS):
        at = pl.ds(i * rows, rows)
        out[at] = jnp.dot(column[at], panel[...], preferred_element_type=F32).astype(BF16)
    if copy:
        copy.wait()


def lower(column_block, panel, kept=None):
    n, k = column_block.shape
    half = panel.shape[1]
    first = kept is None
    return pl.pallas_call(
        lower_kernel,
        out_shape=(shape(n, half),) + (() if first else (shape(n, 2 * half),)),
        in_specs=[ON_CHIP] * (2 if first else 3),
        out_specs=(ON_CHIP,) + (() if first else (IN_HBM,)),
        scratch_shapes=[] if first else [pltpu.SemaphoreType.DMA],
        compiler_params=PARAMS,
        cost_estimate=cost(WEIGHT * 2 * n * k * half, 2 * (n * k + k * half + n * half)),
        name="lower_own" if first else "lower_other",
    )(column_block, panel, *(() if first else (kept,)))


def schur_kernel(own_lower, own_panel, other_lower, other_panel, coupling, _, lower_out, out, done, out_sems, lower_sem):
    half = own_lower.shape[1]
    cols = pl.ds(pl.multiple_of((1 - my_core()) * half, 128), half)
    copies = [pltpu.make_async_copy(other_lower, lower_out.at[:, cols], lower_sem)]
    copies[-1].start()
    contract = (((1,), (1,)), ((), ()))
    start = 0
    for i, rows in enumerate(schur_chunks(coupling.shape[0])):
        at = pl.ds(start, rows)
        product = lax.dot_general(own_lower[at], own_panel[...], contract, preferred_element_type=F32)
        product += lax.dot_general(other_lower[at], other_panel[...], contract, preferred_element_type=F32)
        done[at] = (coupling[at].astype(F32) - product).astype(BF16)
        copies.append(pltpu.make_async_copy(done.at[at], out.at[at], out_sems.at[i]))
        copies[-1].start()
        start += rows
    for copy in copies:
        copy.wait()


def schur_chunks(rows):
    quarter = rows // 4
    return [quarter, quarter, quarter, quarter // 2, quarter // 2]


def schur(own_lower, own_panel, other_lower, other_panel, coupling, so_far):
    n, cols = coupling.shape
    k = 2 * own_lower.shape[1]
    return pl.pallas_call(
        schur_kernel,
        out_shape=(shape(n, k), shape(n, cols)),
        in_specs=[ON_CHIP] * 5 + [IN_HBM],
        out_specs=(IN_HBM, IN_HBM),
        scratch_shapes=[
            pltpu.VMEM((n, cols), BF16),
            pltpu.SemaphoreType.DMA((len(schur_chunks(n)),)),
            pltpu.SemaphoreType.DMA,
        ],
        input_output_aliases={5: 0},
        compiler_params=PARAMS,
        cost_estimate=cost(2 * n * k * cols, 2 * (n * k + k * cols + 2 * n * cols)),
        name="schur",
    )(own_lower, own_panel, other_lower, other_panel, coupling, so_far)


def on_device(devices, coupling, column_block, pivot_inverse, row_panel):
    chips = devices // 2
    steps = chips // 2
    ring = ring_of(chips)
    over = [(i, i ^ 1) for i in range(devices)]
    up = [(2 * ring[i] + c, 2 * ring[(i + 1) % chips] + c) for i in range(chips) for c in range(2)]
    down = [(to, at) for at, to in up]
    send = lambda x, to: lax.ppermute(x, "row", to)
    p_rows, r_rows = pivot_inverse.shape[0], row_panel.shape[1]

    mine, theirs = split(pivot_inverse, row_panel.T)
    rising = [mine, send(theirs, over)]
    falling = list(rising)
    pieces = [(rising[s], 0, s) for s in range(2)]
    for k in range(1, steps):
        for s in range(2):
            rising[s], falling[s] = send(rising[s], up), send(falling[s], down)
            pieces += [(rising[s], -k, s), (falling[s], k, s)]
        if k == 1:
            column_block, coupling = fetch(after(column_block, rising[0]), coupling)
    last = [send(rising[0], up), send(falling[1], down)]
    rows = p_rows + r_rows
    early = send(stack([(x, 0, rows) for x, _, _ in pieces], "early"), over)
    late = send(stack([(x, 0, rows) for x in last], "late"), over)
    own = [(x, 0, d, s) for x, d, s in pieces] + [(last[s], 0, steps, s) for s in range(2)]
    other = [(early, i * rows, d, s) for i, (_, d, s) in enumerate(pieces)]
    other += [(late, s * rows, steps, s) for s in range(2)]
    below = lambda parts: [(x, start + p_rows, d, s) for x, start, d, s in parts]

    own_p = place(own, p_rows, chips, 0, "place_own_p")
    (own_lower,) = lower(column_block, own_p)
    other_p = place(other, p_rows, chips, 1, "place_other_p")
    other_lower, lower_panel = lower(column_block, other_p, own_lower)
    own_r = place(below(own), r_rows, chips, 0, "place_own_r")
    other_r = place(below(other), r_rows, chips, 1, "place_other_r")
    return schur(own_lower, own_r, other_lower, other_r, coupling, lower_panel)


def by_all_gather(coupling, column_block, pivot_inverse, row_panel):
    whole_inverse = lax.all_gather(pivot_inverse, "row", axis=0, tiled=True)
    whole_panel = lax.all_gather(row_panel, "row", axis=1, tiled=True)
    lower_panel = jnp.dot(column_block, whole_inverse, preferred_element_type=F32).astype(BF16)
    product = jnp.dot(lower_panel, whole_panel, preferred_element_type=F32)
    return lower_panel, (coupling.astype(F32) - product).astype(BF16)


def solution(mesh):
    devices = mesh.shape["row"]
    parts = mesh.shape["groups"]

    def step(coupling, column_block, pivot_inverse, row_panel):
        fits = devices % 4 == 0 and devices >= 8
        fits &= row_panel.shape[1] // (parts * devices) % 8 == 0
        fits &= pivot_inverse.shape[0] // (parts * devices) % 8 == 0
        body = functools.partial(on_device, devices) if fits else by_all_gather
        rows = P(("groups", "row"), None)
        return jax.shard_map(
            body,
            mesh=mesh,
            in_specs=(rows, rows, rows, P(None, ("groups", "row"))),
            out_specs=(rows, rows),
            check_vma=False,
        )(coupling, column_block, pivot_inverse, row_panel)

    return step
```

```python
import functools

import jax
import jax.numpy as jnp
from jax import lax
from jax.experimental import pallas as pl
from jax.experimental.pallas import tpu as pltpu
from jax.sharding import PartitionSpec as P

F32, BF16 = jnp.float32, jnp.bfloat16
ON_CHIP = pl.BlockSpec(memory_space=pltpu.VMEM)
IN_HBM = pl.BlockSpec(memory_space=pltpu.HBM)
PARAMS = pltpu.CompilerParams(vmem_limit_bytes=16 << 20)
CHUNKS = 4
WEIGHT = 20
FETCH_AT = 2
MARK = 10_000_000_000


def shape(*dims):
    return jax.ShapeDtypeStruct(dims, BF16)


def cost(flops, nbytes):
    return pl.CostEstimate(flops=flops, bytes_accessed=nbytes, transcendentals=0)


def small(kernel, out_shape, operands, name):
    return pl.pallas_call(
        kernel,
        out_shape=out_shape,
        in_specs=[ON_CHIP] * len(operands),
        out_specs=jax.tree.map(lambda _: ON_CHIP, out_shape),
        compiler_params=PARAMS,
        name=name,
    )(*operands)


def in_hbm(x):
    return pltpu.with_memory_space_constraint(x, pltpu.HBM)


def after(value, *others):
    return lax.optimization_barrier((value, *others))[0]


def ring_of(chips):
    if chips > 8:
        return list(range(chips))
    return list(range(0, chips, 2)) + list(range(chips - 1, 0, -2))


def chip_at(distance, chips):
    chip = lax.axis_index("row") // 2
    if chips > 8:
        return lax.rem(chip + distance + chips, chips)
    place = jnp.where(lax.rem(chip, 2) == 0, chip // 2, chips - 1 - chip // 2)
    place = lax.rem(place + distance + chips, chips)
    return jnp.where(place < chips // 2, 2 * place, 2 * (chips - 1 - place) + 1)


def my_core():
    return lax.rem(lax.axis_index("row"), 2)


def part_of(rows):
    return -(-rows // 16) * 8


def stack(parts, name):
    sizes = [part_of(rows) if mine else rows for _, _, rows, mine in parts]

    def kernel(*refs):
        to = 0
        for ref, (_, start, rows, mine), size in zip(refs, parts, sizes):
            taken = ref[start : start + size]
            if mine:
                taken = jnp.where(my_core() == 0, taken, ref[start + rows - size : start + rows])
            refs[-1][to : to + size] = taken
            to += size

    return small(kernel, shape(sum(sizes), parts[0][0].shape[1]), [part[0] for part in parts], name)


def place(parts, rows, chips, name):
    def kernel(*refs):
        core = my_core()
        for ref, (_, start, steps, stream, side) in zip(refs, parts):
            by = core if side == 0 else 1 - core
            chip = chip_at(jnp.where(by == 0, -steps, steps), chips)
            at = (2 * chip + (by if stream == 0 else 1 - by)) * rows
            size = rows
            if 2 * steps == chips:
                size = part_of(rows)
                at += by * (rows - size)
            refs[-1][pl.ds(pl.multiple_of(at, 8), size), :] = ref[start : start + size]

    cols = parts[0][0].shape[1]
    return small(kernel, shape(2 * chips * rows, cols), [part[0] for part in parts], name)


def mark(piece):
    def kernel(piece_ref, out):
        out[...] = piece_ref[:16, :128]

    return pl.pallas_call(
        kernel,
        out_shape=shape(16, 128),
        in_specs=[ON_CHIP],
        out_specs=ON_CHIP,
        compiler_params=PARAMS,
        cost_estimate=cost(MARK, 0),
        name="mark",
    )(piece)


def fetch_kernel(*refs):
    count = len(refs) // 2
    copies = [pltpu.make_async_copy(refs[i], refs[count + i], refs[-1].at[i]) for i in range(count)]
    for copy in copies:
        copy.start()
    for copy in copies:
        copy.wait()


def fetch(*arrays):
    return pl.pallas_call(
        fetch_kernel,
        out_shape=tuple(shape(*x.shape) for x in arrays),
        in_specs=[IN_HBM] * len(arrays),
        out_specs=(ON_CHIP,) * len(arrays),
        scratch_shapes=[pltpu.SemaphoreType.DMA((len(arrays),))],
        compiler_params=PARAMS,
        name="fetch",
    )(*map(in_hbm, arrays))


def lower_kernel(part, column, panel, out):
    rows, half = column.shape[0] // CHUNKS, out.shape[1]
    for i in range(CHUNKS):
        at = pl.ds(i * rows, rows)
        out[at] = jnp.dot(
            column[at], panel[:, part * half : (part + 1) * half], preferred_element_type=F32
        ).astype(BF16)


def lower(column_block, panel, part):
    n, k = column_block.shape
    half = panel.shape[1] // 2
    return pl.pallas_call(
        functools.partial(lower_kernel, part),
        out_shape=shape(n, half),
        in_specs=[ON_CHIP, ON_CHIP],
        out_specs=ON_CHIP,
        compiler_params=PARAMS,
        cost_estimate=cost(WEIGHT * 2 * n * k * half, 2 * (n * k + k * half + n * half)),
        name="lower",
    )(column_block, panel)


def schur_kernel(left, right, panel, coupling, lower_out, out, done, out_sems, lower_sems):
    half = left.shape[1]
    copies = []
    for i, ref in enumerate((left, right)):
        copies.append(pltpu.make_async_copy(ref, lower_out.at[:, pl.ds(i * half, half)], lower_sems.at[i]))
        copies[-1].start()
    contract = (((1,), (1,)), ((), ()))
    rows = coupling.shape[0] // CHUNKS
    for i in range(CHUNKS):
        at = pl.ds(i * rows, rows)
        product = lax.dot_general(left[at], panel[:, :half], contract, preferred_element_type=F32)
        product += lax.dot_general(right[at], panel[:, half:], contract, preferred_element_type=F32)
        done[at] = (coupling[at].astype(F32) - product).astype(BF16)
        copies.append(pltpu.make_async_copy(done.at[at], out.at[at], out_sems.at[i]))
        copies[-1].start()
    for copy in copies:
        copy.wait()


def schur(left, right, panel, coupling):
    n, cols = coupling.shape
    k = 2 * left.shape[1]
    return pl.pallas_call(
        schur_kernel,
        out_shape=(shape(n, k), shape(n, cols)),
        in_specs=[ON_CHIP] * 4,
        out_specs=(IN_HBM, IN_HBM),
        scratch_shapes=[
            pltpu.VMEM((n, cols), BF16),
            pltpu.SemaphoreType.DMA((CHUNKS,)),
            pltpu.SemaphoreType.DMA((2,)),
        ],
        compiler_params=PARAMS,
        cost_estimate=cost(2 * n * k * cols, 2 * (2 * n * k + k * cols + 2 * n * cols)),
        name="schur",
    )(left, right, panel, coupling)


def on_device(devices, coupling, column_block, pivot_inverse, row_panel):
    chips = devices // 2
    steps = chips // 2
    ring = ring_of(chips)
    swap = [(i, i ^ 1) for i in range(devices)]
    hops = [(ring[i], ring[(i + 1) % chips]) for i in range(chips)]
    along = [(2 * a, 2 * b) for a, b in hops] + [(2 * b + 1, 2 * a + 1) for a, b in hops]
    on = lambda x: lax.ppermute(x, "row", along)
    over = lambda x: lax.ppermute(x, "row", swap)
    p_rows, r_rows = pivot_inverse.shape[0], row_panel.shape[1]

    p_start = [pivot_inverse, over(pivot_inverse)]
    (row_panel,) = fetch(row_panel.T)
    r_start = [row_panel, over(row_panel)]
    p_parts = [(p_start[s], 0, 0, s, 0) for s in range(2)]
    r_parts = [(r_start[s], 0, 0, s, 0) for s in range(2)]

    def keep(x, k, s, p_at, r_at):
        for side, y in enumerate((x, over(x))):
            if p_at is not None:
                p_parts.append((y, p_at, k, s, side))
            if r_at is not None:
                r_parts.append((y, r_at, k - 1, s, side))

    held = p_start
    for k in range(1, steps):
        held = [on(x) for x in held]
        for s in range(2):
            keep(held[s], k, s, 0, p_rows if k > 1 else None)
        held[1] = after(held[1], mark(held[0]))
        if k == 1:
            held = [stack([(held[s], 0, p_rows, False), (r_start[s], 0, r_rows, False)], "follow") for s in range(2)]
        if k == FETCH_AT:
            column_block, coupling = fetch(after(column_block, held[0]), coupling)
            held[1] = after(held[1], column_block)
    held = [on(stack([(x, 0, p_rows, True), (x, p_rows, r_rows, False)], "opposite_p")) for x in held]
    for s in range(2):
        keep(held[s], steps, s, 0, part_of(p_rows))
    held[1] = after(held[1], mark(held[0]))
    last = on(stack([(x, part_of(p_rows), r_rows, True) for x in held], "opposite_r"))

    panel = place(p_parts, p_rows, chips, "place_p")
    left = lower(column_block, panel, 0)
    for side, x in enumerate((last, over(after(last, left)))):
        r_parts += [(x, s * part_of(r_rows), steps, s, side) for s in range(2)]
    right = lower(column_block, after(panel, last), 1)
    return schur(left, right, place(r_parts, r_rows, chips, "place_r"), coupling)


def by_all_gather(coupling, column_block, pivot_inverse, row_panel):
    whole_inverse = lax.all_gather(pivot_inverse, "row", axis=0, tiled=True)
    whole_panel = lax.all_gather(row_panel, "row", axis=1, tiled=True)
    lower_panel = jnp.dot(column_block, whole_inverse, preferred_element_type=F32).astype(BF16)
    product = jnp.dot(lower_panel, whole_panel, preferred_element_type=F32)
    return lower_panel, (coupling.astype(F32) - product).astype(BF16)


def solution(mesh):
    devices = mesh.shape["row"]
    parts = mesh.shape["groups"]

    def step(coupling, column_block, pivot_inverse, row_panel):
        fits = devices % 4 == 0 and devices >= 12
        fits &= row_panel.shape[1] // (parts * devices) % 8 == 0
        fits &= pivot_inverse.shape[0] // (parts * devices) % 8 == 0
        body = functools.partial(on_device, devices) if fits else by_all_gather
        rows = P(("groups", "row"), None)
        return jax.shard_map(
            body,
            mesh=mesh,
            in_specs=(rows, rows, rows, P(None, ("groups", "row"))),
            out_specs=(rows, rows),
            check_vma=False,
        )(coupling, column_block, pivot_inverse, row_panel)

    return step
```

```python
import functools
import math

import jax
import jax.numpy as jnp
from jax import lax
from jax.experimental import pallas as pl
from jax.experimental.pallas import tpu as pltpu
from jax.sharding import PartitionSpec as P

F32, BF16 = jnp.float32, jnp.bfloat16
ON_CHIP = pl.BlockSpec(memory_space=pltpu.VMEM)
IN_HBM = pl.BlockSpec(memory_space=pltpu.HBM)
PARAMS = pltpu.CompilerParams(vmem_limit_bytes=20 << 20)
CHUNKS = 4
WEIGHT = 20
MARK = 10_000_000_000


def shape(*dims):
    return jax.ShapeDtypeStruct(dims, BF16)


def cost(flops, nbytes):
    return pl.CostEstimate(flops=flops, bytes_accessed=nbytes, transcendentals=0)


def small(kernel, out_shape, operands, name):
    return pl.pallas_call(
        kernel,
        out_shape=out_shape,
        in_specs=[ON_CHIP] * len(operands),
        out_specs=jax.tree.map(lambda _: ON_CHIP, out_shape),
        compiler_params=PARAMS,
        name=name,
    )(*operands)


def in_hbm(x):
    return pltpu.with_memory_space_constraint(x, pltpu.HBM)


def after(value, *others):
    return lax.optimization_barrier((value, *others))[0]


def ring_of(chips):
    if chips > 8:
        return list(range(chips))
    return list(range(0, chips, 2)) + list(range(chips - 1, 0, -2))


def chip_at(distance, chips):
    chip = lax.axis_index("row") // 2
    if chips > 8:
        return lax.rem(chip + distance + chips, chips)
    place = jnp.where(lax.rem(chip, 2) == 0, chip // 2, chips - 1 - chip // 2)
    place = lax.rem(place + distance + chips, chips)
    return jnp.where(place < chips // 2, 2 * place, 2 * (chips - 1 - place) + 1)


def my_core():
    return lax.rem(lax.axis_index("row"), 2)


def owner_row(rows, chips, steps, stream, side):
    by = my_core() if side == 0 else 1 - my_core()
    chip = chip_at(jnp.where(by == 0, -steps, steps), chips)
    return (2 * chip + (by if stream == 0 else 1 - by)) * rows


def place(parts, rows, chips, zero, name):
    def kernel(*refs):
        out = refs[-1]
        for ref, (_, start, *origin) in zip(refs, parts):
            at = pl.multiple_of(owner_row(rows, chips, *origin), 8)
            out[pl.ds(at, rows), :] = ref[start : start + rows]
        if zero:
            at = pl.multiple_of(2 * chip_at(chips // 2, chips) * rows, 8)
            out[pl.ds(at, 2 * rows), :] = jnp.zeros((2 * rows, out.shape[1]), BF16)

    cols = parts[0][0].shape[1]
    return small(kernel, shape(2 * chips * rows, cols), [part[0] for part in parts], name)


def window_of(rows, chips):
    chunk, whole = 2 * rows, 2 * rows * chips
    size = min(-(-(chunk + 128 - math.gcd(chunk, 128)) // 128) * 128, whole)
    start = chip_at(chips // 2, chips) * chunk // 128 * 128
    return pl.multiple_of(jnp.minimum(start, whole - size), 128), size


def opposite(p_parts, p_rows, r_parts, r_rows, r_panel, chips):
    _, size = window_of(p_rows, chips)
    parts = p_parts + r_parts
    cols = r_panel.shape[1]

    def kernel(*refs):
        window, panel = refs[-2:]
        first, _ = window_of(p_rows, chips)
        window[...] = jnp.zeros_like(window)
        for i, (ref, (_, start, *origin)) in enumerate(zip(refs, parts)):
            rows, out = (p_rows, window) if i < len(p_parts) else (r_rows, panel)
            at = owner_row(rows, chips, *origin)
            at = at - first if i < len(p_parts) else at
            out[pl.ds(pl.multiple_of(at, 8), rows), :] = ref[start : start + rows]

    return pl.pallas_call(
        kernel,
        out_shape=(shape(size, cols), shape(*r_panel.shape)),
        in_specs=[ON_CHIP] * (len(parts) + 1),
        out_specs=(ON_CHIP, ON_CHIP),
        input_output_aliases={len(parts): 1},
        compiler_params=PARAMS,
        name="opposite",
    )(*[part[0] for part in parts], r_panel)


def load_kernel(inverse, panel, out, sems):
    rows = inverse.shape[0]
    copies = [
        pltpu.make_async_copy(inverse, out.at[pl.ds(0, rows)], sems.at[0]),
        pltpu.make_async_copy(panel, out.at[pl.ds(rows, panel.shape[0])], sems.at[1]),
    ]
    for copy in copies:
        copy.start()
    for copy in copies:
        copy.wait()


def load(inverse, panel):
    return pl.pallas_call(
        load_kernel,
        out_shape=shape(inverse.shape[0] + panel.shape[0], inverse.shape[1]),
        in_specs=[IN_HBM, IN_HBM],
        out_specs=ON_CHIP,
        scratch_shapes=[pltpu.SemaphoreType.DMA((2,))],
        compiler_params=PARAMS,
        name="load",
    )(in_hbm(inverse), in_hbm(panel))


def mark(piece):
    def kernel(piece_ref, out):
        out[...] = piece_ref[:16, :128]

    return pl.pallas_call(
        kernel,
        out_shape=shape(16, 128),
        in_specs=[ON_CHIP],
        out_specs=ON_CHIP,
        compiler_params=PARAMS,
        cost_estimate=cost(MARK, 0),
        name="mark",
    )(piece)


def lower_kernel(column, panel, out):
    rows = column.shape[0] // CHUNKS
    for i in range(CHUNKS):
        at = pl.ds(i * rows, rows)
        out[at] = jnp.dot(column[at], panel[...], preferred_element_type=F32)


def lower(column_block, panel):
    n, k = column_block.shape
    return pl.pallas_call(
        lower_kernel,
        out_shape=jax.ShapeDtypeStruct((n, panel.shape[1]), F32),
        in_specs=[ON_CHIP, ON_CHIP],
        out_specs=ON_CHIP,
        compiler_params=PARAMS,
        cost_estimate=cost(WEIGHT * 2 * n * k * k, 2 * (n * k + k * k + 2 * n * k)),
        name="lower",
    )(column_block, panel)


def finish_kernel(p_rows, chips, so_far, column, window, panel, coupling, lower_out, out, lower_done, done, sems):
    first, size = window_of(p_rows, chips)
    contract = (((1,), (1,)), ((), ()))
    rows = coupling.shape[0] // CHUNKS
    copies = []
    for i in range(CHUNKS):
        at = pl.ds(i * rows, rows)
        rest = jnp.dot(column[at, pl.ds(first, size)], window[...], preferred_element_type=F32)
        lower_done[at] = (so_far[at] + rest).astype(BF16)
        copies.append(pltpu.make_async_copy(lower_done.at[at], lower_out.at[at], sems.at[0, i]))
        copies[-1].start()
        product = lax.dot_general(lower_done[at], panel[...], contract, preferred_element_type=F32)
        done[at] = (coupling[at].astype(F32) - product).astype(BF16)
        copies.append(pltpu.make_async_copy(done.at[at], out.at[at], sems.at[1, i]))
        copies[-1].start()
    for copy in copies:
        copy.wait()


def finish(so_far, column_block, window, panel, coupling, p_rows, chips):
    n, cols = coupling.shape
    k = so_far.shape[1]
    return pl.pallas_call(
        functools.partial(finish_kernel, p_rows, chips),
        out_shape=(shape(n, k), shape(n, cols)),
        in_specs=[ON_CHIP] * 5,
        out_specs=(IN_HBM, IN_HBM),
        scratch_shapes=[
            pltpu.VMEM((n, k), BF16),
            pltpu.VMEM((n, cols), BF16),
            pltpu.SemaphoreType.DMA((2, CHUNKS)),
        ],
        compiler_params=PARAMS,
        cost_estimate=cost(2 * n * k * (cols + 256), 2 * (4 * n * k + k * cols + 2 * n * cols)),
        name="finish",
    )(so_far, column_block, window, panel, coupling)


def on_device(devices, coupling, column_block, pivot_inverse, row_panel):
    chips = devices // 2
    steps = chips // 2
    ring = ring_of(chips)
    swap = [(i, i ^ 1) for i in range(devices)]
    hops = [(ring[i], ring[(i + 1) % chips]) for i in range(chips)]
    along = [(2 * a, 2 * b) for a, b in hops] + [(2 * b + 1, 2 * a + 1) for a, b in hops]
    on = lambda x: lax.ppermute(x, "row", along)
    over = lambda x: lax.ppermute(x, "row", swap)
    p_rows, r_rows = pivot_inverse.shape[0], row_panel.shape[1]

    shards = load(pivot_inverse, row_panel.T)
    held = [shards, over(shards)]
    pieces = [(held[s], 0, s, 0) for s in range(2)]
    for k in range(1, steps):
        held = [on(x) for x in held]
        pieces += [(y, k, s, side) for s in range(2) for side, y in enumerate((held[s], over(held[s])))]
        held[1] = after(held[1], mark(held[0]))
    last = on(held[0])

    at = lambda start, some: [(x, start, *origin) for x, *origin in some]
    panel = place(at(0, pieces), p_rows, chips, True, "place_p")
    r_panel = place(at(p_rows, pieces), r_rows, chips, False, "place_r")
    so_far = lower(column_block, panel)
    parts = [(last, steps, 0, 0), (over(after(last, so_far)), steps, 0, 1)]
    p_parts, r_parts = at(0, parts), at(p_rows, parts)
    window, r_panel = opposite(p_parts, p_rows, r_parts, r_rows, r_panel, chips)
    return finish(so_far, column_block, window, r_panel, coupling, p_rows, chips)


def by_all_gather(coupling, column_block, pivot_inverse, row_panel):
    whole_inverse = lax.all_gather(pivot_inverse, "row", axis=0, tiled=True)
    whole_panel = lax.all_gather(row_panel, "row", axis=1, tiled=True)
    lower_panel = jnp.dot(column_block, whole_inverse, preferred_element_type=F32).astype(BF16)
    product = jnp.dot(lower_panel, whole_panel, preferred_element_type=F32)
    return lower_panel, (coupling.astype(F32) - product).astype(BF16)


def solution(mesh):
    devices = mesh.shape["row"]
    parts = mesh.shape["groups"]

    def step(coupling, column_block, pivot_inverse, row_panel):
        fits = devices % 4 == 0 and devices >= 12
        fits &= row_panel.shape[1] // (parts * devices) % 8 == 0
        fits &= pivot_inverse.shape[0] // (parts * devices) % 8 == 0
        body = functools.partial(on_device, devices) if fits else by_all_gather
        rows = P(("groups", "row"), None)
        return jax.shard_map(
            body,
            mesh=mesh,
            in_specs=(rows, rows, rows, P(None, ("groups", "row"))),
            out_specs=(rows, rows),
            check_vma=False,
        )(coupling, column_block, pivot_inverse, row_panel)

    return step
```

```python
import functools
import math

import jax
import jax.numpy as jnp
from jax import lax
from jax.experimental import pallas as pl
from jax.experimental.pallas import tpu as pltpu
from jax.sharding import PartitionSpec as P

F32, BF16 = jnp.float32, jnp.bfloat16
ON_CHIP = pl.BlockSpec(memory_space=pltpu.VMEM)
IN_HBM = pl.BlockSpec(memory_space=pltpu.HBM)
PARAMS = pltpu.CompilerParams(vmem_limit_bytes=20 << 20)
CHUNKS = 4
WEIGHT = 20
MARK = 10_000_000_000


def shape(*dims):
    return jax.ShapeDtypeStruct(dims, BF16)


def cost(flops, nbytes):
    return pl.CostEstimate(flops=flops, bytes_accessed=nbytes, transcendentals=0)


def small(kernel, out_shape, operands, name):
    return pl.pallas_call(
        kernel,
        out_shape=out_shape,
        in_specs=[ON_CHIP] * len(operands),
        out_specs=jax.tree.map(lambda _: ON_CHIP, out_shape),
        compiler_params=PARAMS,
        name=name,
    )(*operands)


def in_hbm(x):
    return pltpu.with_memory_space_constraint(x, pltpu.HBM)


def after(value, *others):
    return lax.optimization_barrier((value, *others))[0]


def ring_of(chips):
    if chips > 8:
        return list(range(chips))
    return list(range(0, chips, 2)) + list(range(chips - 1, 0, -2))


def chip_at(distance, chips):
    chip = lax.axis_index("row") // 2
    if chips > 8:
        return lax.rem(chip + distance + chips, chips)
    place = jnp.where(lax.rem(chip, 2) == 0, chip // 2, chips - 1 - chip // 2)
    place = lax.rem(place + distance + chips, chips)
    return jnp.where(place < chips // 2, 2 * place, 2 * (chips - 1 - place) + 1)


def my_core():
    return lax.rem(lax.axis_index("row"), 2)


def owner_row(rows, chips, steps, stream, side):
    by = my_core() if side == 0 else 1 - my_core()
    chip = chip_at(jnp.where(by == 0, -steps, steps), chips)
    return (2 * chip + (by if stream == 0 else 1 - by)) * rows


def place(parts, rows, chips, zero, name):
    def kernel(*refs):
        out = refs[-1]
        for ref, (_, start, *origin) in zip(refs, parts):
            at = pl.multiple_of(owner_row(rows, chips, *origin), 8)
            out[pl.ds(at, rows), :] = ref[start : start + rows]
        if zero:
            at = pl.multiple_of(2 * chip_at(chips // 2, chips) * rows, 8)
            out[pl.ds(at, 2 * rows), :] = jnp.zeros((2 * rows, out.shape[1]), BF16)

    cols = parts[0][0].shape[1]
    return small(kernel, shape(2 * chips * rows, cols), [part[0] for part in parts], name)


def window_of(rows, chips):
    chunk, whole = 2 * rows, 2 * rows * chips
    size = min(-(-(chunk + 128 - math.gcd(chunk, 128)) // 128) * 128, whole)
    start = chip_at(chips // 2, chips) * chunk // 128 * 128
    return pl.multiple_of(jnp.minimum(start, whole - size), 128), size


def opposite(p_parts, p_rows, r_parts, r_rows, r_panel, chips):
    _, size = window_of(p_rows, chips)
    parts = p_parts + r_parts
    cols = r_panel.shape[1]

    def kernel(*refs):
        window, panel = refs[-2:]
        first, _ = window_of(p_rows, chips)
        window[...] = jnp.zeros_like(window)
        for i, (ref, (_, start, *origin)) in enumerate(zip(refs, parts)):
            rows, out = (p_rows, window) if i < len(p_parts) else (r_rows, panel)
            at = owner_row(rows, chips, *origin)
            at = at - first if i < len(p_parts) else at
            out[pl.ds(pl.multiple_of(at, 8), rows), :] = ref[start : start + rows]

    return pl.pallas_call(
        kernel,
        out_shape=(shape(size, cols), shape(*r_panel.shape)),
        in_specs=[ON_CHIP] * (len(parts) + 1),
        out_specs=(ON_CHIP, ON_CHIP),
        input_output_aliases={len(parts): 1},
        compiler_params=PARAMS,
        name="opposite",
    )(*[part[0] for part in parts], r_panel)


def load_kernel(inverse, panel, out, sems):
    rows = inverse.shape[0]
    copies = [
        pltpu.make_async_copy(inverse, out.at[pl.ds(0, rows)], sems.at[0]),
        pltpu.make_async_copy(panel, out.at[pl.ds(rows, panel.shape[0])], sems.at[1]),
    ]
    for copy in copies:
        copy.start()
    for copy in copies:
        copy.wait()


def load(inverse, panel):
    return pl.pallas_call(
        load_kernel,
        out_shape=shape(inverse.shape[0] + panel.shape[0], inverse.shape[1]),
        in_specs=[IN_HBM, IN_HBM],
        out_specs=ON_CHIP,
        scratch_shapes=[pltpu.SemaphoreType.DMA((2,))],
        compiler_params=PARAMS,
        name="load",
    )(in_hbm(inverse), in_hbm(panel))


def mark(piece):
    def kernel(piece_ref, out):
        out[...] = piece_ref[:16, :128]

    return pl.pallas_call(
        kernel,
        out_shape=shape(16, 128),
        in_specs=[ON_CHIP],
        out_specs=ON_CHIP,
        compiler_params=PARAMS,
        cost_estimate=cost(MARK, 0),
        name="mark",
    )(piece)


def lower_kernel(column, panel, out):
    rows = column.shape[0] // CHUNKS
    for i in range(CHUNKS):
        at = pl.ds(i * rows, rows)
        out[at] = jnp.dot(column[at], panel[...], preferred_element_type=F32)


def lower(column_block, panel):
    n, k = column_block.shape
    return pl.pallas_call(
        lower_kernel,
        out_shape=jax.ShapeDtypeStruct((n, panel.shape[1]), F32),
        in_specs=[ON_CHIP, ON_CHIP],
        out_specs=ON_CHIP,
        compiler_params=PARAMS,
        cost_estimate=cost(WEIGHT * 2 * n * k * k, 2 * (n * k + k * k + 2 * n * k)),
        name="lower",
    )(column_block, panel)


def finish_kernel(p_rows, chips, so_far, column, window, panel, coupling, lower_out, out, lower_done, done, sems):
    first, size = window_of(p_rows, chips)
    contract = (((1,), (1,)), ((), ()))
    rows = coupling.shape[0] // CHUNKS
    copies = []
    for i in range(CHUNKS):
        at = pl.ds(i * rows, rows)
        rest = jnp.dot(column[at, pl.ds(first, size)], window[...], preferred_element_type=F32)
        lower_done[at] = (so_far[at] + rest).astype(BF16)
        copies.append(pltpu.make_async_copy(lower_done.at[at], lower_out.at[at], sems.at[0, i]))
        copies[-1].start()
        cols = out.shape[1]
        cuts = [0, (cols // 2 + 127) // 256 * 256, cols] if i == CHUNKS - 1 else [0, cols]
        for j, (low, high) in enumerate(zip(cuts, cuts[1:])):
            product = lax.dot_general(lower_done[at], panel[low:high], contract, preferred_element_type=F32)
            done[at, low:high] = (coupling[at, low:high].astype(F32) - product).astype(BF16)
            columns = pl.ds(low, high - low)
            copies.append(
                pltpu.make_async_copy(done.at[at, columns], out.at[at, columns], sems.at[1 + j, i])
            )
            copies[-1].start()
    for copy in copies:
        copy.wait()


def finish(so_far, column_block, window, panel, coupling, p_rows, chips):
    n, cols = coupling.shape
    k = so_far.shape[1]
    return pl.pallas_call(
        functools.partial(finish_kernel, p_rows, chips),
        out_shape=(shape(n, k), shape(n, cols)),
        in_specs=[ON_CHIP] * 5,
        out_specs=(IN_HBM, IN_HBM),
        scratch_shapes=[
            pltpu.VMEM((n, k), BF16),
            pltpu.VMEM((n, cols), BF16),
            pltpu.SemaphoreType.DMA((3, CHUNKS)),
        ],
        compiler_params=PARAMS,
        cost_estimate=cost(2 * n * k * (cols + 256), 2 * (4 * n * k + k * cols + 2 * n * cols)),
        name="finish",
    )(so_far, column_block, window, panel, coupling)


def on_device(devices, coupling, column_block, pivot_inverse, row_panel):
    chips = devices // 2
    steps = chips // 2
    ring = ring_of(chips)
    swap = [(i, i ^ 1) for i in range(devices)]
    hops = [(ring[i], ring[(i + 1) % chips]) for i in range(chips)]
    along = [(2 * a, 2 * b) for a, b in hops] + [(2 * b + 1, 2 * a + 1) for a, b in hops]
    on = lambda x: lax.ppermute(x, "row", along)
    over = lambda x: lax.ppermute(x, "row", swap)
    p_rows, r_rows = pivot_inverse.shape[0], row_panel.shape[1]

    shards = load(pivot_inverse, row_panel.T)
    held = [shards, over(shards)]
    pieces = [(held[s], 0, s, 0) for s in range(2)]
    for k in range(1, steps):
        held = [on(x) for x in held]
        pieces += [(y, k, s, side) for s in range(2) for side, y in enumerate((held[s], over(held[s])))]
        held[1] = after(held[1], mark(held[0]))
    last = on(held[0])

    at = lambda start, some: [(x, start, *origin) for x, *origin in some]
    panel = place(at(0, pieces), p_rows, chips, True, "place_p")
    r_panel = place(at(p_rows, pieces), r_rows, chips, False, "place_r")
    so_far = lower(column_block, panel)
    parts = [(last, steps, 0, 0), (over(after(last, so_far)), steps, 0, 1)]
    p_parts, r_parts = at(0, parts), at(p_rows, parts)
    window, r_panel = opposite(p_parts, p_rows, r_parts, r_rows, r_panel, chips)
    return finish(so_far, column_block, window, r_panel, coupling, p_rows, chips)


def by_all_gather(coupling, column_block, pivot_inverse, row_panel):
    whole_inverse = lax.all_gather(pivot_inverse, "row", axis=0, tiled=True)
    whole_panel = lax.all_gather(row_panel, "row", axis=1, tiled=True)
    lower_panel = jnp.dot(column_block, whole_inverse, preferred_element_type=F32).astype(BF16)
    product = jnp.dot(lower_panel, whole_panel, preferred_element_type=F32)
    return lower_panel, (coupling.astype(F32) - product).astype(BF16)


def solution(mesh):
    devices = mesh.shape["row"]
    parts = mesh.shape["groups"]

    def step(coupling, column_block, pivot_inverse, row_panel):
        fits = devices % 4 == 0 and devices >= 12
        fits &= row_panel.shape[1] // (parts * devices) % 8 == 0
        fits &= pivot_inverse.shape[0] // (parts * devices) % 8 == 0
        body = functools.partial(on_device, devices) if fits else by_all_gather
        rows = P(("groups", "row"), None)
        return jax.shard_map(
            body,
            mesh=mesh,
            in_specs=(rows, rows, rows, P(None, ("groups", "row"))),
            out_specs=(rows, rows),
            check_vma=False,
        )(coupling, column_block, pivot_inverse, row_panel)

    return step
```

```python
import functools
import math

import jax
import jax.numpy as jnp
from jax import lax
from jax.experimental import pallas as pl
from jax.experimental.pallas import tpu as pltpu
from jax.sharding import PartitionSpec as P

F32, BF16 = jnp.float32, jnp.bfloat16
ON_CHIP = pl.BlockSpec(memory_space=pltpu.VMEM)
IN_HBM = pl.BlockSpec(memory_space=pltpu.HBM)
PARAMS = pltpu.CompilerParams(vmem_limit_bytes=20 << 20)
CHUNKS = 4
WEIGHT = 20
MARK = 10_000_000_000


def shape(*dims):
    return jax.ShapeDtypeStruct(dims, BF16)


def cost(flops, nbytes):
    return pl.CostEstimate(flops=flops, bytes_accessed=nbytes, transcendentals=0)


def small(kernel, out_shape, operands, name):
    return pl.pallas_call(
        kernel,
        out_shape=out_shape,
        in_specs=[ON_CHIP] * len(operands),
        out_specs=jax.tree.map(lambda _: ON_CHIP, out_shape),
        compiler_params=PARAMS,
        name=name,
    )(*operands)


def in_hbm(x):
    return pltpu.with_memory_space_constraint(x, pltpu.HBM)


def after(value, *others):
    return lax.optimization_barrier((value, *others))[0]


def ring_of(chips):
    if chips > 8:
        return list(range(chips))
    return list(range(0, chips, 2)) + list(range(chips - 1, 0, -2))


def chip_at(distance, chips):
    chip = lax.axis_index("row") // 2
    if chips > 8:
        return lax.rem(chip + distance + chips, chips)
    place = jnp.where(lax.rem(chip, 2) == 0, chip // 2, chips - 1 - chip // 2)
    place = lax.rem(place + distance + chips, chips)
    return jnp.where(place < chips // 2, 2 * place, 2 * (chips - 1 - place) + 1)


def my_core():
    return lax.rem(lax.axis_index("row"), 2)


def owner_row(rows, chips, steps, stream, side):
    by = my_core() if side == 0 else 1 - my_core()
    chip = chip_at(jnp.where(by == 0, -steps, steps), chips)
    return (2 * chip + (by if stream == 0 else 1 - by)) * rows


def place(parts, rows, chips, zero, name):
    def kernel(*refs):
        out = refs[-1]
        for ref, (_, start, *origin) in zip(refs, parts):
            at = pl.multiple_of(owner_row(rows, chips, *origin), 8)
            out[pl.ds(at, rows), :] = ref[start : start + rows]
        if zero:
            at = pl.multiple_of(2 * chip_at(chips // 2, chips) * rows, 8)
            out[pl.ds(at, 2 * rows), :] = jnp.zeros((2 * rows, out.shape[1]), BF16)

    cols = parts[0][0].shape[1]
    return small(kernel, shape(2 * chips * rows, cols), [part[0] for part in parts], name)


def window_of(rows, chips):
    chunk, whole = 2 * rows, 2 * rows * chips
    size = min(-(-(chunk + 128 - math.gcd(chunk, 128)) // 128) * 128, whole)
    start = chip_at(chips // 2, chips) * chunk // 128 * 128
    return pl.multiple_of(jnp.minimum(start, whole - size), 128), size


def opposite(p_parts, p_rows, r_parts, r_rows, r_panel, chips):
    _, size = window_of(p_rows, chips)
    parts = p_parts + r_parts
    cols = r_panel.shape[1]

    def kernel(*refs):
        window, panel = refs[-2:]
        first, _ = window_of(p_rows, chips)
        window[...] = jnp.zeros_like(window)
        for i, (ref, (_, start, *origin)) in enumerate(zip(refs, parts)):
            rows, out = (p_rows, window) if i < len(p_parts) else (r_rows, panel)
            at = owner_row(rows, chips, *origin)
            at = at - first if i < len(p_parts) else at
            out[pl.ds(pl.multiple_of(at, 8), rows), :] = ref[start : start + rows]

    return pl.pallas_call(
        kernel,
        out_shape=(shape(size, cols), shape(*r_panel.shape)),
        in_specs=[ON_CHIP] * (len(parts) + 1),
        out_specs=(ON_CHIP, ON_CHIP),
        input_output_aliases={len(parts): 1},
        compiler_params=PARAMS,
        name="opposite",
    )(*[part[0] for part in parts], r_panel)


def load_kernel(inverse, panel, out, sems):
    rows = inverse.shape[0]
    copies = [
        pltpu.make_async_copy(inverse, out.at[pl.ds(0, rows)], sems.at[0]),
        pltpu.make_async_copy(panel, out.at[pl.ds(rows, panel.shape[0])], sems.at[1]),
    ]
    for copy in copies:
        copy.start()
    for copy in copies:
        copy.wait()


def load(inverse, panel):
    return pl.pallas_call(
        load_kernel,
        out_shape=shape(inverse.shape[0] + panel.shape[0], inverse.shape[1]),
        in_specs=[IN_HBM, IN_HBM],
        out_specs=ON_CHIP,
        scratch_shapes=[pltpu.SemaphoreType.DMA((2,))],
        compiler_params=PARAMS,
        name="load",
    )(in_hbm(inverse), in_hbm(panel))


def mark(piece):
    def kernel(piece_ref, out):
        out[...] = piece_ref[:16, :128]

    return pl.pallas_call(
        kernel,
        out_shape=shape(16, 128),
        in_specs=[ON_CHIP],
        out_specs=ON_CHIP,
        compiler_params=PARAMS,
        cost_estimate=cost(MARK, 0),
        name="mark",
    )(piece)


def lower_kernel(column, panel, out):
    rows = column.shape[0] // CHUNKS
    for i in range(CHUNKS):
        at = pl.ds(i * rows, rows)
        out[at] = jnp.dot(column[at], panel[...], preferred_element_type=F32)


def lower(column_block, panel):
    n, k = column_block.shape
    return pl.pallas_call(
        lower_kernel,
        out_shape=jax.ShapeDtypeStruct((n, panel.shape[1]), F32),
        in_specs=[ON_CHIP, ON_CHIP],
        out_specs=ON_CHIP,
        compiler_params=PARAMS,
        cost_estimate=cost(WEIGHT * 2 * n * k * k, 2 * (n * k + k * k + 2 * n * k)),
        name="lower",
    )(column_block, panel)


def finish_kernel(p_rows, chips, so_far, column, window, panel, coupling, lower_out, out, lower_done, done, sems):
    first, size = window_of(p_rows, chips)
    contract = (((1,), (1,)), ((), ()))
    rows = coupling.shape[0] // CHUNKS
    copies = []
    for i in range(CHUNKS):
        at = pl.ds(i * rows, rows)
        rest = jnp.dot(column[at, pl.ds(first, size)], window[...], preferred_element_type=F32)
        lower_done[at] = (so_far[at] + rest).astype(BF16)
        copies.append(pltpu.make_async_copy(lower_done.at[at], lower_out.at[at], sems.at[0, i]))
        copies[-1].start()
    for i in range(CHUNKS):
        at = pl.ds(i * rows, rows)
        cols = out.shape[1]
        cuts = [0, (cols // 2 + 127) // 256 * 256, cols] if i == CHUNKS - 1 else [0, cols]
        for j, (low, high) in enumerate(zip(cuts, cuts[1:])):
            product = lax.dot_general(lower_done[at], panel[low:high], contract, preferred_element_type=F32)
            done[at, low:high] = (coupling[at, low:high].astype(F32) - product).astype(BF16)
            columns = pl.ds(low, high - low)
            copies.append(
                pltpu.make_async_copy(done.at[at, columns], out.at[at, columns], sems.at[1 + j, i])
            )
            copies[-1].start()
    for copy in copies:
        copy.wait()


def finish(so_far, column_block, window, panel, coupling, p_rows, chips):
    n, cols = coupling.shape
    k = so_far.shape[1]
    return pl.pallas_call(
        functools.partial(finish_kernel, p_rows, chips),
        out_shape=(shape(n, k), shape(n, cols)),
        in_specs=[ON_CHIP] * 5,
        out_specs=(IN_HBM, IN_HBM),
        scratch_shapes=[
            pltpu.VMEM((n, k), BF16),
            pltpu.VMEM((n, cols), BF16),
            pltpu.SemaphoreType.DMA((3, CHUNKS)),
        ],
        compiler_params=PARAMS,
        cost_estimate=cost(2 * n * k * (cols + 256), 2 * (4 * n * k + k * cols + 2 * n * cols)),
        name="finish",
    )(so_far, column_block, window, panel, coupling)


def on_device(devices, coupling, column_block, pivot_inverse, row_panel):
    chips = devices // 2
    steps = chips // 2
    ring = ring_of(chips)
    swap = [(i, i ^ 1) for i in range(devices)]
    hops = [(ring[i], ring[(i + 1) % chips]) for i in range(chips)]
    along = [(2 * a, 2 * b) for a, b in hops] + [(2 * b + 1, 2 * a + 1) for a, b in hops]
    on = lambda x: lax.ppermute(x, "row", along)
    over = lambda x: lax.ppermute(x, "row", swap)
    p_rows, r_rows = pivot_inverse.shape[0], row_panel.shape[1]

    shards = load(pivot_inverse, row_panel.T)
    held = [shards, over(shards)]
    pieces = [(held[s], 0, s, 0) for s in range(2)]
    for k in range(1, steps):
        held = [on(x) for x in held]
        pieces += [(y, k, s, side) for s in range(2) for side, y in enumerate((held[s], over(held[s])))]
        held[1] = after(held[1], mark(held[0]))
    last = on(held[0])

    at = lambda start, some: [(x, start, *origin) for x, *origin in some]
    panel = place(at(0, pieces), p_rows, chips, True, "place_p")
    r_panel = place(at(p_rows, pieces), r_rows, chips, False, "place_r")
    so_far = lower(column_block, panel)
    parts = [(last, steps, 0, 0), (over(after(last, so_far)), steps, 0, 1)]
    p_parts, r_parts = at(0, parts), at(p_rows, parts)
    window, r_panel = opposite(p_parts, p_rows, r_parts, r_rows, r_panel, chips)
    return finish(so_far, column_block, window, r_panel, coupling, p_rows, chips)


def by_all_gather(coupling, column_block, pivot_inverse, row_panel):
    whole_inverse = lax.all_gather(pivot_inverse, "row", axis=0, tiled=True)
    whole_panel = lax.all_gather(row_panel, "row", axis=1, tiled=True)
    lower_panel = jnp.dot(column_block, whole_inverse, preferred_element_type=F32).astype(BF16)
    product = jnp.dot(lower_panel, whole_panel, preferred_element_type=F32)
    return lower_panel, (coupling.astype(F32) - product).astype(BF16)


def solution(mesh):
    devices = mesh.shape["row"]
    parts = mesh.shape["groups"]

    def step(coupling, column_block, pivot_inverse, row_panel):
        fits = devices % 4 == 0 and devices >= 12
        fits &= row_panel.shape[1] // (parts * devices) % 8 == 0
        fits &= pivot_inverse.shape[0] // (parts * devices) % 8 == 0
        body = functools.partial(on_device, devices) if fits else by_all_gather
        rows = P(("groups", "row"), None)
        return jax.shard_map(
            body,
            mesh=mesh,
            in_specs=(rows, rows, rows, P(None, ("groups", "row"))),
            out_specs=(rows, rows),
            check_vma=False,
        )(coupling, column_block, pivot_inverse, row_panel)

    return step
```
